32 devices in a mesh: rep: 2 (over y), seq: 16 (over z, x, core).
Axes of the slice: x: 2, y: 2, z: 4, core: 2. Of those that a mesh axis runs over, the one named last changes fastest.
Arguments:
- latents: bfloat16 [16, 24576], P(None, ('rep', 'seq')), parts along dimension 1, may hold values from -6 to 6
- layout: int32 [32, 768], P('rep'), parts along dimension 0, may hold values from 0 to 12287, as said below
- assign: int32 [16], P('rep'), parts along dimension 0, may hold values from 0 to 7, as said below
- counts: int32 [16], P('rep'), parts along dimension 0, may hold values from 1 to 3
- latent_cache: bfloat16 [2, 128, 1024], P(None, ('rep', 'seq')), parts along dimension 1, may hold values from -6 to 6
- feature_cache: bfloat16 [2, 128, 64, 384], P(None, ('rep', 'seq')), parts along dimension 1, may hold values from -4 to 4
- first_weight: bfloat16 [3, 3, 3, 16, 384], replicated, may hold values from -0.3125 to 0.3125
- first_bias: float32 [384], replicated, may hold values from -3 to 3
- norm_gain: float32 [384], replicated, may hold values from 0.25 to 1.75
- second_weight: bfloat16 [3, 3, 3, 384, 192], replicated, may hold values from -0.0625 to 0.0625
- second_bias: float32 [192], replicated, may hold values from -3 to 3
Outputs:
- decoded_frames: bfloat16 [3, 256, 128, 192], P(None, ('rep', 'seq')), parts along dimension 1
- latent_cache_next: bfloat16 [2, 128, 1024], P(None, ('rep', 'seq')), parts along dimension 1
- feature_cache_next: bfloat16 [2, 128, 64, 384], P(None, ('rep', 'seq')), parts along dimension 1
The draws below stay inside these ranges and needn't reach their ends.
There are 2 independent parts, one for each index of `rep`. The reference program is written for one: setup_inputs(seed, part) draws one part's arguments, and reference() takes and returns one part's arrays. A program takes and returns all parts, laid end to end along the dimension named above; an argument that names none is the same for every part. Nothing has to cross between parts.
Inputs may be any that keep to these rules, and one draw needn't show every extreme that they name: assign is a permutation of 0 to 7. layout is a permutation of 0 to 12287. Call the cells of request assign[g], rows k * 4 to (k + 1) * 4 - 1, all frames and columns, the tile of seq index (g * 2 + k - 1) mod 16; every row of layout holds exactly 48 cells of every tile.
All inputs are finite; a program needn't handle non-finite values.
Results may differ from the reference program's by a relative error of at most 0.0034.
Values may be sent and summed in bfloat16 or wider, within the bound.
A program may use at most 128 MiB of HBM per device.

```python
import jax
import jax.numpy as jnp
from jax import lax

LAT_CH = 16
MID_CH = 384
OUT_CH = 192
REQS = 8
FMAX = 3
ROWS_DEV = 4
W = 64
GROUP = 2
SHIFT = 1
HEIGHT = 8
CELLS = 768
PEER = 48
TOTAL_CELLS = 12288
ROWS_ALL = 64
N_SEQ = 16


def pairing(key):
    return jax.random.permutation(jax.random.fold_in(key, 11), REQS).astype(jnp.int32)


def one_permutation(subkey):
    return jax.random.permutation(subkey, CELLS).astype(jnp.int32)


def draw_assign(key, part):
    return pairing(key)


def draw_layout(key, part):
    assign = pairing(key)
    spread_keys = jax.random.split(jax.random.fold_in(key, 23), N_SEQ)
    within = jax.vmap(one_permutation)(spread_keys)
    numbers = jnp.arange(N_SEQ, dtype=jnp.int32)[:, None] * CELLS + within
    numbers = jnp.transpose(numbers.reshape(N_SEQ, N_SEQ, PEER), (1, 0, 2)).reshape(N_SEQ, CELLS)
    slot_keys = jax.random.split(jax.random.fold_in(key, 37), N_SEQ)
    mixing = jax.vmap(one_permutation)(slot_keys)
    numbers = jnp.take_along_axis(numbers, mixing, axis=1)
    target = numbers // CELLS
    inside = numbers % CELLS
    frame_index = inside // (ROWS_DEV * W)
    tile_row = inside // W % ROWS_DEV
    column = inside % W
    place = (target + SHIFT) % N_SEQ
    group_index = place // GROUP
    position = place % GROUP
    request = jnp.take(assign, group_index)
    image_row = position * ROWS_DEV + tile_row
    return (((request * FMAX + frame_index) * HEIGHT + image_row) * W + column).astype(jnp.int32)


def plant(entries, key, smallest, top_value):
    spot = [jax.random.randint(jax.random.fold_in(key, axis), (), 0, length) for axis, length in enumerate(entries.shape)]
    longest = entries.shape.index(max(entries.shape))
    neighbour = spot[:longest] + [(spot[longest] + 1) % entries.shape[longest]] + spot[longest + 1:]
    return entries.at[tuple(spot)].set(smallest).at[tuple(neighbour)].set(top_value)


def levels(rng, extent, cuts, low, largest):
    factor_of = 1.0
    for axis_at, blocks in cuts:
        draws = jax.random.uniform(jax.random.fold_in(jax.random.fold_in(rng, 6), axis_at), (blocks,), jnp.float32, low / len(cuts), largest / len(cuts))
        factor_of = factor_of * jnp.repeat(jnp.exp(draws), extent[axis_at] // blocks).reshape((-1,) + (1,) * (len(extent) - 1 - axis_at))
    return factor_of


def scatter_about(key, shape, deviation, bound, pieces=(), kind=jnp.bfloat16):
    values = jax.random.normal(key, shape, jnp.float32) * deviation
    if len(pieces) > 0:
        values = levels(key, shape, pieces, -0.22, 0.18) * values
    return jnp.clip(values, min=-bound, max=bound).astype(kind)


def setup_inputs(seed: int = 0, part: int = 0) -> dict:
    key_of = jax.random.split(jax.random.key(seed), 12)
    part_keys = jax.random.split(jax.random.fold_in(key_of[11], part), 12)
    return {
        "latents": scatter_about(part_keys[0], (LAT_CH, TOTAL_CELLS), 1.0, 6.0, ((1, 16),)),
        "layout": draw_layout(jax.random.fold_in(jax.random.fold_in(key_of[11], part), 71), part),
        "assign": draw_assign(jax.random.fold_in(jax.random.fold_in(key_of[11], part), 71), part),
        "counts": plant(jax.random.randint(part_keys[3], (REQS,), 1, FMAX + 1), jax.random.fold_in(part_keys[3], 1), 1, FMAX).astype(jnp.int32),
        "latent_cache": scatter_about(part_keys[4], (2, ROWS_ALL, W * LAT_CH), 1.0, 6.0, ((1, 16),)),
        "feature_cache": scatter_about(part_keys[5], (2, ROWS_ALL, W, MID_CH), 0.6, 4.0, ((1, 16),)),
        "first_weight": scatter_about(key_of[6], (3, 3, 3, LAT_CH, MID_CH), (27 * LAT_CH) ** -0.5, 0.3125),
        "first_bias": scatter_about(key_of[7], (MID_CH,), 0.5, 3.0, (), jnp.float32),
        "norm_gain": jnp.clip(1.0 + 0.15 * jax.random.normal(key_of[8], (MID_CH,), jnp.float32), 0.25, 1.75),
        "second_weight": scatter_about(key_of[9], (3, 3, 3, MID_CH, OUT_CH), (27 * MID_CH) ** -0.5, 0.0625),
        "second_bias": scatter_about(key_of[10], (OUT_CH,), 0.5, 3.0, (), jnp.float32),
    }


def causal_conv(values, weight, offset):
    result = lax.conv_general_dilated(values[None], weight, (1, 1, 1), ((0, 0), (1, 1), (1, 1)), dimension_numbers=('NDHWC', 'DHWIO', 'NDHWC'), preferred_element_type=jnp.float32)
    return result[0] + offset

def activate(linear, norm_gain):
    inverse = lax.rsqrt(lax.optimization_barrier(jnp.mean(linear * linear, axis=-1, keepdims=True)) + 1e-06)
    return jax.nn.silu(linear * inverse * norm_gain).astype(jnp.bfloat16)

def reference(latents, layout, assign, counts, latent_cache, feature_cache, first_weight, first_bias, norm_gain, second_weight, second_bias):
    positions = jnp.argsort(layout.reshape(-1)).astype(jnp.int32)
    ordered = jnp.take(latents, positions, axis=1).reshape(LAT_CH, REQS, FMAX, HEIGHT, W)
    ordered = jnp.transpose(ordered, (1, 2, 3, 4, 0))
    latent_prev = jnp.roll(latent_cache, SHIFT * ROWS_DEV, axis=1).reshape(2, REQS, HEIGHT, W, LAT_CH)
    feature_prev = jnp.roll(feature_cache, SHIFT * ROWS_DEV, axis=1).reshape(2, REQS, HEIGHT, W, MID_CH)
    frame_index = jnp.arange(FMAX, dtype=jnp.int32)[:, None, None, None]
    decoded_list = []
    latent_list = []
    feature_list = []
    for group_index in range(REQS):
        request = assign[group_index].astype(jnp.int32)
        live_frames = counts[request].astype(jnp.int32)
        window = lax.dynamic_index_in_dim(ordered, request, 0, keepdims=False)
        first_input = jnp.concatenate([latent_prev[:, group_index], window], axis=0)
        features = activate(causal_conv(first_input, first_weight, first_bias), norm_gain)
        second_input = jnp.concatenate([feature_prev[:, group_index], features], axis=0)
        doubled = jnp.repeat(jnp.repeat(second_input, 2, axis=1), 2, axis=2)
        decoded = causal_conv(doubled, second_weight, second_bias)
        decoded = jnp.where(frame_index < live_frames, decoded, 0.0).astype(jnp.bfloat16)
        decoded_list.append(decoded)
        latent_list.append(lax.dynamic_slice_in_dim(first_input, live_frames, 2, 0))
        feature_list.append(lax.dynamic_slice_in_dim(second_input, live_frames, 2, 0))
    decoded_frames = jnp.roll(jnp.concatenate(decoded_list, axis=1), -2 * SHIFT * ROWS_DEV, axis=1)
    latent_cache_next = jnp.roll(jnp.concatenate(latent_list, axis=1), -SHIFT * ROWS_DEV, axis=1).reshape(2, ROWS_ALL, W * LAT_CH)
    feature_cache_next = jnp.roll(jnp.concatenate(feature_list, axis=1), -SHIFT * ROWS_DEV, axis=1)
    return (decoded_frames, latent_cache_next, feature_cache_next)
```

```python
import jax
import jax.numpy as jnp
from jax import lax
from jax.experimental import pallas as pl
from jax.experimental.pallas import tpu as pltpu
from jax.sharding import PartitionSpec as P

LAT_CH = 16
REQS = 8
FMAX = 3
ROWS_DEV = 4
W = 64


def padded_2(array, sides, width):
    for axis, dim in sides:
        devices, length = (lax.axis_size(axis), array.shape[dim])
        up = [(i, (i + 1) % devices) for i in range(devices)]
        down = [(j, i) for i, j in up]
        last = lax.slice_in_dim(array, length - width, length, axis=dim)
        first = lax.slice_in_dim(array, 0, width, axis=dim)
        before = lax.ppermute(last, axis, up)
        after = lax.ppermute(first, axis, down)
        array = jnp.concatenate([before, array, after], axis=dim)
    return array


def tile_numbers(layout, assign, per_group, devices):
    height = ROWS_DEV * per_group
    offset = per_group // 2
    tile_cells = FMAX * ROWS_DEV * W
    column = layout % W
    remain = layout // W
    image_row = remain % height
    remain = remain // height
    frame_index = remain % FMAX
    request = remain // FMAX
    group_ranks = jnp.arange(REQS, dtype=jnp.int32)
    group_index = jnp.sum(jnp.where(assign == request[..., None], group_ranks, 0), axis=-1)
    place = group_index * per_group + image_row // ROWS_DEV
    target = (place - offset + devices) % devices
    within = (frame_index * ROWS_DEV + image_row % ROWS_DEV) * W + column
    return target * tile_cells + within


def keep_rows(values, rim_width, position, height):
    row_index = position * ROWS_DEV - rim_width + jnp.arange(values.shape[1], dtype=jnp.int32)
    inside = (row_index >= 0) & (row_index < height)
    return jnp.where(inside[None, :, None, None], values, jnp.zeros((), values.dtype))


def causal_conv(values, weight, offset):
    result = lax.conv_general_dilated(
        values[None],
        weight,
        (1, 1, 1),
        ((0, 0), (0, 0), (1, 1)),
        dimension_numbers=("NDHWC", "DHWIO", "NDHWC"),
        preferred_element_type=jnp.float32,
    )
    return result[0] + offset


def activate(linear, norm_gain):
    inverse = lax.rsqrt(jnp.mean(linear * linear, axis=-1, keepdims=True) + 1e-06)
    return jax.nn.silu(linear * inverse * norm_gain).astype(jnp.bfloat16)


def decode_kernel(info, cached, fresh, weight, bias, out, carry, shifted, packed, even, odd):
    frame = pl.program_id(0)
    rows, columns, mid = fresh.shape[1:]
    width = bias.shape[-1]
    lanes = packed.shape[-1]
    history = cached.shape[0]

    @pl.when(frame == 0)
    def _prepare():
        def pack(step, _):
            at = pl.multiple_of(step * 16, 16)
            for a in range(3):
                taps = [
                    [weight[a, b, e, pl.ds(at, 16), :].astype(jnp.float32) for e in range(3)]
                    for b in range(3)
                ]
                for py in range(2):
                    if py == 0:
                        lines = (taps[0], [taps[1][e] + taps[2][e] for e in range(3)])
                    else:
                        lines = ([taps[0][e] + taps[1][e] for e in range(3)], taps[2])
                    for px in range(2):
                        for iy, line in enumerate(lines):
                            if px == 0:
                                pair = (line[0], line[1] + line[2])
                            else:
                                pair = (line[0] + line[1], line[2])
                            for ix, value in enumerate(pair):
                                start = ((a * 2 + iy) * 2 + ix) * mid
                                packed[2 * py + px, pl.ds(start + at, 16), 0:width] = value.astype(
                                    jnp.bfloat16
                                )
                                packed[2 * py + px, pl.ds(start + at, 16), width:lanes] = jnp.zeros(
                                    (16, lanes - width), jnp.bfloat16
                                )
            return 0

        lax.fori_loop(0, mid // 16, pack, 0)
        edge = lax.broadcasted_iota(jnp.int32, (columns, mid), 0)
        for source, count, first in ((cached, history, 0), (fresh, fresh.shape[0], history)):
            def shift(step, _):
                f = step // rows
                r = step % rows
                bad = ((r == 0) & (info[0] == 0)) | ((r == rows - 1) & (info[1] == 0))
                value = jnp.where(bad, 0.0, source[f, r].astype(jnp.float32))
                left = jnp.where(edge == 0, 0.0, pltpu.roll(value, 1, 0))
                right = jnp.where(edge == columns - 1, 0.0, pltpu.roll(value, columns - 1, 0))
                shifted[0, first + f, r] = left.astype(jnp.bfloat16)
                shifted[1, first + f, r] = value.astype(jnp.bfloat16)
                shifted[2, first + f, r] = right.astype(jnp.bfloat16)
                return 0

            lax.fori_loop(0, count * rows, shift, 0)
        for i in range(history):
            carry[i] = shifted[1, info[2] + i, 1 : rows - 1]

    inner = rows - 2
    cells = inner * columns
    live = frame < info[2]
    for py in range(2):
        for px in range(2):
            parts = []
            for a in range(3):
                for iy in range(2):
                    for ix in range(2):
                        block = shifted[px + ix, frame + a, py + iy : py + iy + inner]
                        parts.append(block.reshape(cells, mid))
            total = jnp.dot(
                jnp.concatenate(parts, axis=1),
                packed[2 * py + px],
                preferred_element_type=jnp.float32,
            )
            even[pl.ds(px, cells, stride=2), :] = total[:, 0:128]
            odd[pl.ds(px, cells, stride=2), :] = total[:, 128:256]
        for i in range(inner):
            span = pl.ds(i * 2 * columns, 2 * columns)
            low = even[span, :] + bias[:, 0:128]
            high = odd[span, 0 : width - 128] + bias[:, 128:width]
            out[0, 2 * i + py, :, 0:128] = jnp.where(live, low, 0.0).astype(jnp.bfloat16)
            out[0, 2 * i + py, :, 128:width] = jnp.where(live, high, 0.0).astype(jnp.bfloat16)


def decode(info, cached, fresh, weight, bias):
    history, rows, columns, mid = cached.shape
    width = bias.shape[-1]
    inner = rows - 2
    frames = fresh.shape[0]
    lanes = 256
    return pl.pallas_call(
        decode_kernel,
        grid=(frames,),
        in_specs=[
            pl.BlockSpec(memory_space=pltpu.SMEM),
            pl.BlockSpec(cached.shape, lambda t: (0, 0, 0, 0)),
            pl.BlockSpec(fresh.shape, lambda t: (0, 0, 0, 0)),
            pl.BlockSpec(weight.shape, lambda t: (0, 0, 0, 0, 0)),
            pl.BlockSpec((1, width), lambda t: (0, 0)),
        ],
        out_specs=[
            pl.BlockSpec((1, 2 * inner, 2 * columns, width), lambda t: (t, 0, 0, 0)),
            pl.BlockSpec((history, inner, columns, mid), lambda t: (0, 0, 0, 0)),
        ],
        out_shape=[
            jax.ShapeDtypeStruct((frames, 2 * inner, 2 * columns, width), jnp.bfloat16),
            jax.ShapeDtypeStruct((history, inner, columns, mid), jnp.bfloat16),
        ],
        scratch_shapes=[
            pltpu.VMEM((3, history + frames, rows, columns, mid), jnp.bfloat16),
            pltpu.VMEM((4, 12 * mid, lanes), jnp.bfloat16),
            pltpu.VMEM((2 * inner * columns, 128), jnp.float32),
            pltpu.VMEM((2 * inner * columns, 128), jnp.float32),
        ],
        compiler_params=pltpu.CompilerParams(
            dimension_semantics=("arbitrary",), vmem_limit_bytes=56 * 1024 * 1024
        ),
        cost_estimate=pl.CostEstimate(
            flops=2 * frames * inner * columns * 48 * mid * lanes,
            bytes_accessed=8_000_000,
            transcendentals=0,
        ),
    )(info, cached, fresh, weight, bias[None])


def one_hot(values, count, dtype=jnp.bfloat16):
    return (values[..., None] == jnp.arange(count, dtype=jnp.int32)).astype(dtype)


def body(
    latents,
    layout,
    assign,
    counts,
    latent_cache,
    feature_cache,
    first_weight,
    first_bias,
    norm_gain,
    second_weight,
    second_bias,
):
    devices = lax.axis_size("seq")
    myself = lax.axis_index("seq")
    per_group = devices // REQS
    offset = per_group // 2
    height = ROWS_DEV * per_group
    tile_cells = FMAX * ROWS_DEV * W
    per_peer = tile_cells // devices
    numbers = tile_numbers(layout, assign, per_group, devices)
    own_numbers = lax.dynamic_index_in_dim(numbers, myself, 0, keepdims=False)
    send_rank = jnp.sum((own_numbers[None, :] < own_numbers[:, None]).astype(jnp.int32), axis=1)
    outgoing = jnp.dot(latents, one_hot(send_rank, tile_cells)).reshape(LAT_CH, devices, per_peer)
    incoming = lax.all_to_all(outgoing, "seq", split_axis=1, concat_axis=1, tiled=True)
    inside = numbers - myself * tile_cells
    mine = (inside >= 0) & (inside < tile_cells)
    line = jnp.where(mine, inside // W, -1)
    held = jnp.einsum(
        "sph,spl->shl",
        one_hot(line, FMAX * ROWS_DEV),
        one_hot(inside % W, W),
        preferred_element_type=jnp.float32,
    ).reshape(devices, tile_cells)
    cell = jnp.arange(tile_cells, dtype=jnp.int32)
    before = jnp.dot(
        held.astype(jnp.bfloat16),
        (cell[:, None] < cell[None, :]).astype(jnp.bfloat16),
        preferred_element_type=jnp.float32,
    )
    base = jnp.arange(devices, dtype=jnp.float32)[:, None] * per_peer
    slot = jnp.sum(held * (before + base), axis=0).astype(jnp.int32)
    arranged = jnp.dot(
        incoming.reshape(LAT_CH, tile_cells),
        (cell[:, None] == slot[None, :]).astype(jnp.bfloat16),
    )
    window = jnp.transpose(arranged.reshape(LAT_CH, FMAX, ROWS_DEV, W), (1, 2, 3, 0))
    place = (myself + offset) % devices
    position = place % per_group
    request = jnp.take(assign, place // per_group)
    live_frames = jnp.take(counts, request)
    first_input = jnp.concatenate([latent_cache.reshape(2, ROWS_DEV, W, LAT_CH), window], axis=0)
    padded = keep_rows(padded_2(first_input, (("seq", 1),), 2), 2, position, height)
    widened = activate(causal_conv(padded, first_weight, first_bias), norm_gain)
    cached = padded_2(feature_cache, (("seq", 1),), 1)
    info = jnp.stack(
        [
            (position > 0).astype(jnp.int32),
            (position < per_group - 1).astype(jnp.int32),
            live_frames.astype(jnp.int32),
        ]
    )
    decoded_frames, feature_next = decode(info, cached, widened, second_weight, second_bias)
    latent_next = lax.dynamic_slice_in_dim(first_input, live_frames, 2, 0).reshape(
        2, ROWS_DEV, W * LAT_CH
    )
    return (decoded_frames, latent_next, feature_next)


def solution(mesh):
    return jax.shard_map(
        body,
        mesh=mesh,
        in_specs=(
            P(None, ("rep", "seq")),
            P("rep", None),
            P("rep"),
            P("rep"),
            P(None, ("rep", "seq"), None),
            P(None, ("rep", "seq"), None, None),
            P(),
            P(),
            P(),
            P(),
            P(),
        ),
        out_specs=(
            P(None, ("rep", "seq"), None, None),
            P(None, ("rep", "seq"), None),
            P(None, ("rep", "seq"), None, None),
        ),
        check_vma=False,
    )
```

```python
import jax
import jax.numpy as jnp
from jax import lax
from jax.experimental import pallas as pl
from jax.experimental.pallas import tpu as pltpu
from jax.sharding import PartitionSpec as P

LAT_CH = 16
REQS = 8
FMAX = 3
ROWS_DEV = 4
W = 64


def padded_2(array, sides, width):
    for axis, dim in sides:
        devices, length = (lax.axis_size(axis), array.shape[dim])
        up = [(i, (i + 1) % devices) for i in range(devices)]
        down = [(j, i) for i, j in up]
        last = lax.slice_in_dim(array, length - width, length, axis=dim)
        first = lax.slice_in_dim(array, 0, width, axis=dim)
        before = lax.ppermute(last, axis, up)
        after = lax.ppermute(first, axis, down)
        array = jnp.concatenate([before, array, after], axis=dim)
    return array


def tile_numbers(layout, assign, per_group, devices):
    height = ROWS_DEV * per_group
    offset = per_group // 2
    tile_cells = FMAX * ROWS_DEV * W
    column = layout % W
    remain = layout // W
    image_row = remain % height
    remain = remain // height
    frame_index = remain % FMAX
    request = remain // FMAX
    group_ranks = jnp.arange(REQS, dtype=jnp.int32)
    group_index = jnp.sum(jnp.where(assign == request[..., None], group_ranks, 0), axis=-1)
    place = group_index * per_group + image_row // ROWS_DEV
    target = (place - offset + devices) % devices
    within = (frame_index * ROWS_DEV + image_row % ROWS_DEV) * W + column
    return target * tile_cells + within


def keep_rows(values, rim_width, position, height):
    row_index = position * ROWS_DEV - rim_width + jnp.arange(values.shape[1], dtype=jnp.int32)
    inside = (row_index >= 0) & (row_index < height)
    return jnp.where(inside[None, :, None, None], values, jnp.zeros((), values.dtype))


def causal_conv(values, weight, offset):
    result = lax.conv_general_dilated(
        values[None],
        weight,
        (1, 1, 1),
        ((0, 0), (0, 0), (1, 1)),
        dimension_numbers=("NDHWC", "DHWIO", "NDHWC"),
        preferred_element_type=jnp.float32,
    )
    return result[0] + offset


def activate(linear, norm_gain):
    inverse = lax.rsqrt(jnp.mean(linear * linear, axis=-1, keepdims=True) + 1e-06)
    return jax.nn.silu(linear * inverse * norm_gain).astype(jnp.bfloat16)


def decode_kernel(info, cached, fresh, weight, bias, out, carry, shifted, packed):
    frame = pl.program_id(0)
    rows, columns, mid = fresh.shape[1:]
    width = bias.shape[0]
    history = cached.shape[0]

    @pl.when(frame == 0)
    def _prepare():
        def pack(step, _):
            at = pl.multiple_of(step * 16, 16)
            for a in range(3):
                taps = [
                    [weight[a, b, e, pl.ds(at, 16), :].astype(jnp.float32) for e in range(3)]
                    for b in range(3)
                ]
                for py in range(2):
                    if py == 0:
                        lines = (taps[0], [taps[1][e] + taps[2][e] for e in range(3)])
                    else:
                        lines = ([taps[0][e] + taps[1][e] for e in range(3)], taps[2])
                    for px in range(2):
                        for iy, line in enumerate(lines):
                            if px == 0:
                                pair = (line[0], line[1] + line[2])
                            else:
                                pair = (line[0] + line[1], line[2])
                            for ix, value in enumerate(pair):
                                start = ((a * 2 + iy) * 2 + ix) * mid
                                packed[2 * py + px, pl.ds(at, 16), start : start + mid] = value.astype(
                                    jnp.bfloat16
                                )
            return 0

        lax.fori_loop(0, width // 16, pack, 0)
        edge = lax.broadcasted_iota(jnp.int32, (columns, mid), 0)
        for source, count, first in ((cached, history, 0), (fresh, fresh.shape[0], history)):
            def shift(step, _):
                f = step // rows
                r = step % rows
                bad = ((r == 0) & (info[0] == 0)) | ((r == rows - 1) & (info[1] == 0))
                value = jnp.where(bad, 0.0, source[f, r].astype(jnp.float32))
                left = jnp.where(edge == 0, 0.0, pltpu.roll(value, 1, 0))
                right = jnp.where(edge == columns - 1, 0.0, pltpu.roll(value, columns - 1, 0))
                shifted[0, first + f, r] = left.astype(jnp.bfloat16)
                shifted[1, first + f, r] = value.astype(jnp.bfloat16)
                shifted[2, first + f, r] = right.astype(jnp.bfloat16)
                return 0

            lax.fori_loop(0, count * rows, shift, 0)
        for i in range(history):
            carry[i] = shifted[1, info[2] + i, 1 : rows - 1]

    inner = rows - 2
    cells = inner * columns
    live = frame < info[2]
    pair = 2 * columns
    spot = lax.broadcasted_iota(jnp.int32, (2 * pair, 2 * pair), 0)
    goal = spot // pair + 2 * (spot % pair)
    mix = (lax.broadcasted_iota(jnp.int32, (2 * pair, 2 * pair), 1) == goal).astype(jnp.bfloat16)
    for py in range(2):
        halves = []
        for px in range(2):
            parts = []
            for a in range(3):
                for iy in range(2):
                    for ix in range(2):
                        block = shifted[px + ix, frame + a, py + iy : py + iy + inner]
                        parts.append(block.reshape(cells, mid))
            total = lax.dot_general(
                packed[2 * py + px],
                jnp.concatenate(parts, axis=1),
                (((1,), (1,)), ((), ())),
                preferred_element_type=jnp.float32,
            )
            halves.append(jnp.where(live, total + bias[...], 0.0).astype(jnp.bfloat16))
        for i in range(0, inner, 2):
            both = jnp.concatenate(
                [half[:, i * columns : i * columns + pair] for half in halves], axis=1
            )
            mixed = jnp.dot(both, mix, preferred_element_type=jnp.float32).astype(jnp.bfloat16)
            out[0, 2 * i + py] = mixed[:, 0:pair]
            out[0, 2 * i + 2 + py] = mixed[:, pair : 2 * pair]


def decode(info, cached, fresh, weight, bias):
    history, rows, columns, mid = cached.shape
    width = bias.shape[0]
    inner = rows - 2
    frames = fresh.shape[0]
    return pl.pallas_call(
        decode_kernel,
        grid=(frames,),
        in_specs=[
            pl.BlockSpec(memory_space=pltpu.SMEM),
            pl.BlockSpec(cached.shape, lambda t: (0, 0, 0, 0)),
            pl.BlockSpec(fresh.shape, lambda t: (0, 0, 0, 0)),
            pl.BlockSpec(weight.shape, lambda t: (0, 0, 0, 0, 0)),
            pl.BlockSpec((width, 1), lambda t: (0, 0)),
        ],
        out_specs=[
            pl.BlockSpec((1, 2 * inner, width, 2 * columns), lambda t: (t, 0, 0, 0)),
            pl.BlockSpec((history, inner, columns, mid), lambda t: (0, 0, 0, 0)),
        ],
        out_shape=[
            jax.ShapeDtypeStruct((frames, 2 * inner, width, 2 * columns), jnp.bfloat16),
            jax.ShapeDtypeStruct((history, inner, columns, mid), jnp.bfloat16),
        ],
        scratch_shapes=[
            pltpu.VMEM((3, history + frames, rows, columns, mid), jnp.bfloat16),
            pltpu.VMEM((4, width, 12 * mid), jnp.bfloat16),
        ],
        compiler_params=pltpu.CompilerParams(
            dimension_semantics=("arbitrary",), vmem_limit_bytes=56 * 1024 * 1024
        ),
        cost_estimate=pl.CostEstimate(
            flops=2 * frames * inner * columns * 48 * mid * width,
            bytes_accessed=8_000_000,
            transcendentals=0,
        ),
    )(info, cached, fresh, weight, bias[:, None])


def one_hot(values, count, dtype=jnp.bfloat16):
    return (values[..., None] == jnp.arange(count, dtype=jnp.int32)).astype(dtype)


def body(
    latents,
    layout,
    assign,
    counts,
    latent_cache,
    feature_cache,
    first_weight,
    first_bias,
    norm_gain,
    second_weight,
    second_bias,
):
    devices = lax.axis_size("seq")
    myself = lax.axis_index("seq")
    per_group = devices // REQS
    offset = per_group // 2
    height = ROWS_DEV * per_group
    tile_cells = FMAX * ROWS_DEV * W
    per_peer = tile_cells // devices
    numbers = tile_numbers(layout, assign, per_group, devices)
    own_numbers = lax.dynamic_index_in_dim(numbers, myself, 0, keepdims=False)
    send_rank = jnp.sum((own_numbers[None, :] < own_numbers[:, None]).astype(jnp.int32), axis=1)
    outgoing = jnp.dot(latents, one_hot(send_rank, tile_cells)).reshape(LAT_CH, devices, per_peer)
    incoming = lax.all_to_all(outgoing, "seq", split_axis=1, concat_axis=1, tiled=True)
    inside = numbers - myself * tile_cells
    mine = (inside >= 0) & (inside < tile_cells)
    line = jnp.where(mine, inside // W, -1)
    held = jnp.einsum(
        "sph,spl->shl",
        one_hot(line, FMAX * ROWS_DEV),
        one_hot(inside % W, W),
        preferred_element_type=jnp.float32,
    ).reshape(devices, tile_cells)
    cell = jnp.arange(tile_cells, dtype=jnp.int32)
    before = jnp.dot(
        held.astype(jnp.bfloat16),
        (cell[:, None] < cell[None, :]).astype(jnp.bfloat16),
        preferred_element_type=jnp.float32,
    )
    base = jnp.arange(devices, dtype=jnp.float32)[:, None] * per_peer
    slot = jnp.sum(held * (before + base), axis=0).astype(jnp.int32)
    arranged = jnp.dot(
        incoming.reshape(LAT_CH, tile_cells),
        (cell[:, None] == slot[None, :]).astype(jnp.bfloat16),
    )
    window = jnp.transpose(arranged.reshape(LAT_CH, FMAX, ROWS_DEV, W), (1, 2, 3, 0))
    place = (myself + offset) % devices
    position = place % per_group
    request = jnp.take(assign, place // per_group)
    live_frames = jnp.take(counts, request)
    first_input = jnp.concatenate([latent_cache.reshape(2, ROWS_DEV, W, LAT_CH), window], axis=0)
    padded = keep_rows(padded_2(first_input, (("seq", 1),), 2), 2, position, height)
    widened = activate(causal_conv(padded, first_weight, first_bias), norm_gain)
    cached = padded_2(feature_cache, (("seq", 1),), 1)
    info = jnp.stack(
        [
            (position > 0).astype(jnp.int32),
            (position < per_group - 1).astype(jnp.int32),
            live_frames.astype(jnp.int32),
        ]
    )
    decoded_frames, feature_next = decode(
        info, cached, widened, jnp.swapaxes(second_weight, 3, 4), second_bias
    )
    decoded_frames = jnp.swapaxes(decoded_frames, 2, 3)
    latent_next = lax.dynamic_slice_in_dim(first_input, live_frames, 2, 0).reshape(
        2, ROWS_DEV, W * LAT_CH
    )
    return (decoded_frames, latent_next, feature_next)


def solution(mesh):
    return jax.shard_map(
        body,
        mesh=mesh,
        in_specs=(
            P(None, ("rep", "seq")),
            P("rep", None),
            P("rep"),
            P("rep"),
            P(None, ("rep", "seq"), None),
            P(None, ("rep", "seq"), None, None),
            P(),
            P(),
            P(),
            P(),
            P(),
        ),
        out_specs=(
            P(None, ("rep", "seq"), None, None),
            P(None, ("rep", "seq"), None),
            P(None, ("rep", "seq"), None, None),
        ),
        check_vma=False,
    )
```
